32 devices in a mesh: wall: 8 (over y, x, core), vec: 4 (over z).
Axes of the slice: x: 2, y: 2, z: 4, core: 2. Of those that a mesh axis runs over, the one named last changes fastest.
Arguments:
- perturbation: float32 [8, 3, 96, 8, 384], P('vec', None, 'wall'), may hold values from -6 to 6
- prev_term: bfloat16 [8, 3, 96, 8, 384], P('vec', None, 'wall'), may hold values from -6 to 6
- base_store: bfloat16 [8, 3, 96, 8, 384], P('vec', None, 'wall'), may hold values from -4 to 4
- step_index: int32 [1], replicated, may hold values from 0 to 32767
- slot_of_step: int32 [8], replicated, may hold values from 0 to 7, each once
- span_shift: int32 [1], replicated, may hold values from 0 to 383
- lower_gap: float32 [96], P('wall'), may hold values from 0.0005 to 0.012
- pivots: float32 [96], P('wall'), may hold values from 300 to 303
- upper_coef: float32 [96], P('wall'), may hold values from 297 to 300
Outputs:
- advanced: float32 [8, 3, 96, 8, 384], P('vec', None, 'wall')
- advection: bfloat16 [8, 3, 96, 8, 384], P('vec', None, 'wall')
The draws below stay inside these ranges and needn't reach their ends.
Inputs may be any that keep to these rules, and one draw needn't show every extreme that they name: `slot_of_step`: slot s lies at position s % 2 of the steps held by index s // 2 of vec.
All inputs are finite; a program needn't handle non-finite values.
Results may differ from the reference program's by a relative error of at most 0.0025.
Values may be sent and summed in bfloat16 or wider, within the bound.
A program may use at most 64 MiB of HBM per device.

```python
import math
import jax
import jax.numpy as jnp
from jax import lax

NX = 8
NZ = 384
NY = 96
NVEC = 8
STEPS = 8


def block_levels(rng, dims, cuts, least, high):
    gain = 1.0
    for position, parts in cuts:
        steps = jax.random.uniform(jax.random.fold_in(jax.random.fold_in(rng, 6), position), (parts,), jnp.float32, least / len(cuts), high / len(cuts))
        gain = gain * jnp.repeat(jnp.exp(steps), dims[position] // parts).reshape((-1,) + (1,) * (len(dims) - 1 - position))
    return gain


def normal_values(stream_key, extent, deviation, reach, pieces=(), held_as=jnp.bfloat16):
    level = block_levels(stream_key, extent, pieces, -0.22, 0.18) if pieces else 1.0
    result = jax.random.normal(stream_key, extent, jnp.float32) * deviation * level
    return jnp.minimum(jnp.maximum(result, -reach), reach).astype(held_as)


def setup_inputs(seed: int = 0) -> dict:
    key_of = jax.random.split(jax.random.key(seed), 10)
    perturbation = normal_values(key_of[0], (NVEC, 3, NY, NX, NZ), 1.0, 6.0, ((0, 4), (2, 8)), jnp.float32)
    prev_term = normal_values(key_of[1], (NVEC, 3, NY, NX, NZ), 1.0, 6.0, ((0, 4), (2, 8)))
    base_store = normal_values(key_of[2], (STEPS, 3, NY, NX, NZ), 0.7, 4.0, ((0, 4), (2, 8)))
    step_index = jax.random.randint(key_of[3], (1,), 0, STEPS * 4096).astype(jnp.int32)
    slot_of_step = jax.random.permutation(key_of[4], STEPS).astype(jnp.int32)
    span_shift = jax.random.randint(key_of[5], (1,), 0, NZ).astype(jnp.int32)
    lower_gap = jnp.clip(jnp.exp(math.log(0.012) - 3.1780538 * jax.random.uniform(key_of[6], (NY,), jnp.float32) ** block_levels(key_of[6], (NY,), ((0, 8),), -0.2, 0.2)), 0.0005, 0.012)
    pivots = jnp.clip(300.0 + 3.0 * jax.random.uniform(key_of[7], (NY,), jnp.float32) ** block_levels(key_of[7], (NY,), ((0, 8),), -0.2, 0.2), 300.0, 303.0)
    upper_coef = jnp.clip(297.0 + 3.0 * jax.random.uniform(key_of[8], (NY,), jnp.float32) ** block_levels(key_of[8], (NY,), ((0, 8),), -0.2, 0.2), 297.0, 300.0)
    return dict(perturbation=perturbation, prev_term=prev_term, base_store=base_store, step_index=step_index, slot_of_step=slot_of_step, span_shift=span_shift, lower_gap=lower_gap, pivots=pivots, upper_coef=upper_coef)


STEP_SIZE = 0.5
NEW_WEIGHT = 5.0 / 12.0
OLD_WEIGHT = -17.0 / 60.0
VISCOUS_WEIGHT = -0.06


def periodic_diff(field, along):
    return 0.5 * (jnp.roll(field, -1, along) - jnp.roll(field, 1, along))


def reference(perturbation, prev_term, base_store, step_index, slot_of_step, span_shift, lower_gap, pivots, upper_coef):
    step_count = slot_of_step.shape[0]
    orbit_step = (step_index[0] % step_count).astype(jnp.int32)
    slot_index = slot_of_step[orbit_step].astype(jnp.int32)
    chosen = lax.dynamic_index_in_dim(base_store, slot_index, 0, keepdims=False)
    span_cells = chosen.shape[-1]
    doubled = jnp.concatenate([chosen, chosen], axis=3)
    offset = ((span_cells - span_shift[0]) % span_cells).astype(jnp.int32)
    base_field = lax.dynamic_slice_in_dim(doubled, offset, span_cells, 3).astype(jnp.float32)

    def one_vector(inputs):
        vector, previous = inputs
        padded = jnp.pad(vector, ((0, 0), (1, 1), (0, 0), (0, 0)))
        above = padded[:, 2:]
        below = padded[:, :-2]
        explicit = -(base_field[0] * periodic_diff(vector, 2) + base_field[1] * (0.5 * (above - below)) + base_field[2] * periodic_diff(vector, 3))
        source = vector + STEP_SIZE * (NEW_WEIGHT * explicit + OLD_WEIGHT * previous.astype(jnp.float32)) + VISCOUS_WEIGHT * (above - 2.0 * vector + below)
        rows_first = jnp.moveaxis(source, 1, 0)
        start_carry = jnp.zeros(rows_first.shape[1:], jnp.float32)

        def forward(carry, items):
            row_source, gap_value = items
            carry = row_source + (1.0 - gap_value) * carry
            return carry, carry

        _, swept = lax.scan(forward, start_carry, (rows_first, lower_gap))

        def backward(carry, items):
            row_swept, pivot_value, coef_value = items
            carry = (row_swept + coef_value * carry) / pivot_value
            return carry, carry

        _, solved = lax.scan(backward, start_carry, (swept, pivots, upper_coef), reverse=True)
        return jnp.moveaxis(solved, 0, 1), explicit.astype(jnp.bfloat16)

    advanced, advection = lax.map(one_vector, (perturbation, prev_term))
    return advanced, advection
```

```python
import functools

import jax
import jax.numpy as jnp
from jax import lax
from jax.experimental import pallas as pl
from jax.experimental.pallas import tpu as pltpu
from jax.sharding import PartitionSpec as P

STEP_SIZE = 0.5
NEW_WEIGHT = 5.0 / 12.0
OLD_WEIGHT = -17.0 / 60.0
VISCOUS_WEIGHT = -0.06
CHUNK_ROWS = 2
HOP_LAG = 2


def kernel(
    W,
    V,
    q_hbm,
    prev_hbm,
    bs_hbm,
    step_s,
    slots_s,
    shift_s,
    gap_s,
    piv_s,
    up_s,
    adv_hbm,
    advec_hbm,
    qpad,
    prev_v,
    bs_v,
    from_l,
    from_r,
    out_r,
    out_l,
    loc,
    expl,
    adv_v,
    fcar,
    bcar,
    fsend,
    esend,
    cin,
    ctile,
    ctiles,
    tab_d,
    tab_w,
    tab_p,
    tab_rho,
    tab_a,
    tab_c,
    in_sem,
    halo_send,
    halo_recv,
    coef_send,
    coef_recv,
    lr_send,
    lr_recv,
    rl_send,
    rl_recv,
    car_send,
    car_recv,
    out_sem,
):
    w = lax.axis_index("wall")
    v = lax.axis_index("vec")
    nvec, ncomp, rows, nx, nz = q_hbm.shape
    stored = bs_hbm.shape[0]
    fields = nvec * ncomp
    chunks = rows // CHUNK_ROWS

    q_in = pltpu.make_async_copy(q_hbm, qpad.at[:, :, pl.ds(1, rows)], in_sem.at[0])
    prev_in = pltpu.make_async_copy(prev_hbm, prev_v, in_sem.at[1])
    bs_in = pltpu.make_async_copy(bs_hbm, bs_v, in_sem.at[2])
    bs_in.start()
    q_in.start()
    prev_in.start()

    barrier = pltpu.get_barrier_semaphore()
    for s in range(1, W):
        pl.semaphore_signal(
            barrier,
            inc=1,
            device_id={"wall": lax.rem(w + s, W)},
            device_id_type=pl.DeviceIdType.MESH,
        )

    @pl.when(v > 0)
    def _():
        pl.semaphore_signal(
            barrier, inc=1, device_id={"vec": v - 1}, device_id_type=pl.DeviceIdType.MESH
        )

    @pl.when(v < V - 1)
    def _():
        pl.semaphore_signal(
            barrier, inc=1, device_id={"vec": v + 1}, device_id_type=pl.DeviceIdType.MESH
        )

    @pl.when(w == 0)
    def _():
        qpad[:, :, 0] = jnp.zeros((nvec, ncomp, nx, nz), jnp.float32)

    @pl.when(w == W - 1)
    def _():
        qpad[:, :, rows + 1] = jnp.zeros((nvec, ncomp, nx, nz), jnp.float32)

    one = jnp.ones((nx, nz), jnp.float32)

    def down_tables(r, carry):
        prod_d, prod_rho, beta = carry
        d = 1.0 - gap_s[r]
        p = 1.0 / (one * piv_s[r])
        rho = p * up_s[r]
        prod_d = prod_d * d
        weight = prod_rho * p
        tab_d[r] = prod_d
        tab_w[r] = weight
        tab_p[r] = p
        tab_rho[r] = rho
        return prod_d, prod_rho * rho, beta + weight * prod_d

    phi, psi, beta = lax.fori_loop(0, rows, down_tables, (one, one, one * 0.0))
    ctile[0] = phi[:, :128]
    ctile[1] = psi[:, :128]
    ctile[2] = beta[:, :128]

    def up_tables(t, carry):
        a, c = carry
        r = rows - 1 - t
        a = tab_p[r] * tab_d[r] + tab_rho[r] * a
        c = tab_rho[r] * c
        tab_a[r] = a
        tab_c[r] = c
        return a, c

    lax.fori_loop(0, rows, up_tables, (one * 0.0, one))

    neighbours = jnp.where(v > 0, 1, 0) + jnp.where(v < V - 1, 1, 0)
    pl.semaphore_wait(barrier, W - 1 + neighbours)

    def halo_up():
        return pltpu.make_async_remote_copy(
            src_ref=q_hbm.at[:, :, rows - 1],
            dst_ref=qpad.at[:, :, 0],
            send_sem=halo_send.at[0],
            recv_sem=halo_recv.at[0],
            device_id={"wall": w + 1},
            device_id_type=pl.DeviceIdType.MESH,
        )

    def halo_down():
        return pltpu.make_async_remote_copy(
            src_ref=q_hbm.at[:, :, 0],
            dst_ref=qpad.at[:, :, rows + 1],
            send_sem=halo_send.at[1],
            recv_sem=halo_recv.at[1],
            device_id={"wall": w - 1},
            device_id_type=pl.DeviceIdType.MESH,
        )

    def right_copy(k):
        part = pl.ds(k * CHUNK_ROWS, CHUNK_ROWS)
        return pltpu.make_async_remote_copy(
            src_ref=out_r.at[:, part],
            dst_ref=from_l.at[:, part],
            send_sem=lr_send.at[k],
            recv_sem=lr_recv.at[k],
            device_id={"vec": v + 1},
            device_id_type=pl.DeviceIdType.MESH,
        )

    def left_copy(k):
        part = pl.ds(k * CHUNK_ROWS, CHUNK_ROWS)
        return pltpu.make_async_remote_copy(
            src_ref=out_l.at[:, part],
            dst_ref=from_r.at[:, part],
            send_sem=rl_send.at[k],
            recv_sem=rl_recv.at[k],
            device_id={"vec": v - 1},
            device_id_type=pl.DeviceIdType.MESH,
        )

    def coef_copy(s):
        peer = lax.rem(w + s, W)
        return pltpu.make_async_remote_copy(
            src_ref=ctile,
            dst_ref=ctiles.at[w],
            send_sem=coef_send.at[s],
            recv_sem=coef_recv.at[W - s],
            device_id={"wall": peer},
            device_id_type=pl.DeviceIdType.MESH,
        )

    def coef_wait(s):
        pltpu.make_async_copy(ctile, ctiles.at[lax.rem(w + s, W)], coef_recv.at[s]).wait()

    slot = slots_s[lax.rem(step_s[0], slots_s.shape[0])]
    owner = lax.div(slot, stored)
    local = lax.rem(slot, stored)
    mine = owner == v
    before = owner < v
    shift = shift_s[0]

    def own_row(c, y):
        value = bs_v[0, c, y]
        for s in range(1, stored):
            value = jnp.where(local == s, bs_v[s, c, y], value)
        return value

    @pl.when(w < W - 1)
    def _():
        halo_up().start()

    @pl.when(w > 0)
    def _():
        halo_down().start()

    bs_in.wait()

    def each_row(k, body):
        def run(m, carry):
            body(lax.rem(m, ncomp), k * CHUNK_ROWS + lax.div(m, ncomp))
            return carry

        lax.fori_loop(0, ncomp * CHUNK_ROWS, run, 0)

    @pl.when(v == 0)
    def _():
        def go(k, carry):
            def put(c, y):
                out_r[c, y] = own_row(c, y)

            each_row(k, put)
            right_copy(k).start()
            return carry

        lax.fori_loop(0, chunks, go, 0)

    @pl.when(v == V - 1)
    def _():
        def go(k, carry):
            def put(c, y):
                out_l[c, y] = own_row(c, y)

            each_row(k, put)
            left_copy(k).start()
            return carry

        lax.fori_loop(0, chunks, go, 0)

    for s in range(1, W):
        coef_copy(s).start()

    q_in.wait()
    prev_in.wait()

    @pl.when(w < W - 1)
    def _():
        halo_down().wait_recv()

    @pl.when(w > 0)
    def _():
        halo_up().wait_recv()

    fcar[...] = jnp.zeros_like(fcar)
    bcar[...] = jnp.zeros_like(bcar)

    def compute_chunk(k):
        def row(m, carry):
            y = k * CHUNK_ROWS + m
            base = []
            for c in range(ncomp):
                got = jnp.where(before, from_l[c, y], from_r[c, y])
                got = jnp.where(mine, own_row(c, y), got).astype(jnp.float32)
                base.append(pltpu.roll(got, shift, 1))
            d = 1.0 - gap_s[y]
            weight = tab_w[y]

            def field(i, inner):
                n = lax.div(i, ncomp)
                c = lax.rem(i, ncomp)
                mid = qpad[n, c, y + 1]
                above = qpad[n, c, y + 2]
                below = qpad[n, c, y]
                dx = 0.5 * (pltpu.roll(mid, nx - 1, 0) - pltpu.roll(mid, 1, 0))
                dz = 0.5 * (pltpu.roll(mid, nz - 1, 1) - pltpu.roll(mid, 1, 1))
                explicit = -(base[0] * dx + base[1] * (0.5 * (above - below)) + base[2] * dz)
                expl[n, c, y] = explicit.astype(jnp.bfloat16)
                source = (
                    mid
                    + STEP_SIZE
                    * (NEW_WEIGHT * explicit + OLD_WEIGHT * prev_v[n, c, y].astype(jnp.float32))
                    + VISCOUS_WEIGHT * (above - 2.0 * mid + below)
                )
                swept = source + d * fcar[n, c]
                fcar[n, c] = swept
                bcar[n, c] = bcar[n, c] + weight * swept
                loc[n, c, y] = swept
                return inner

            lax.fori_loop(0, fields, field, 0)
            return carry

        lax.fori_loop(0, CHUNK_ROWS, row, 0)

    far = V - 1 - v

    def slot_step(t, carry):
        kl = t - HOP_LAG * v
        kr = t - HOP_LAG * far

        @pl.when((v > 0) & (kl >= 0) & (kl < chunks))
        def _():
            right_copy(kl).wait_recv()

            @pl.when(v < V - 1)
            def _():
                def put(c, y):
                    out_r[c, y] = jnp.where(mine, own_row(c, y), from_l[c, y])

                each_row(kl, put)
                right_copy(kl).start()

        @pl.when((v < V - 1) & (kr >= 0) & (kr < chunks))
        def _():
            left_copy(kr).wait_recv()

            @pl.when(v > 0)
            def _():
                def put(c, y):
                    out_l[c, y] = jnp.where(mine, own_row(c, y), from_r[c, y])

                each_row(kr, put)
                left_copy(kr).start()

        kc = jnp.minimum(kl, kr)

        @pl.when((kc >= 0) & (kc < chunks))
        def _():
            compute_chunk(kc)

        return carry

    lax.fori_loop(0, chunks + HOP_LAG * (V - 1), slot_step, 0)

    advec_out = pltpu.make_async_copy(expl, advec_hbm, out_sem.at[fields])
    advec_out.start()

    for s in range(1, W):
        coef_wait(s)
    ctiles[w] = ctile[...]

    def tail_response(m, total):
        j = W - 1 - m
        tile = ctiles[j]
        new = tile[2] + tile[1] * total * tile[0]
        return jnp.where(j > w, new, total)

    wide = nz // 128

    def widen(x):
        return jnp.concatenate([x] * wide, axis=-1)

    tail = widen(lax.fori_loop(0, W - 1, tail_response, jnp.zeros((nx, 128), jnp.float32)))
    gain = psi * tail

    def pack(i, carry):
        n = lax.div(i, ncomp)
        c = lax.rem(i, ncomp)
        f = fcar[n, c]
        fsend[n, c] = f.astype(jnp.bfloat16)
        esend[n, c] = (bcar[n, c] + gain * f).astype(jnp.bfloat16)
        return carry

    lax.fori_loop(0, fields, pack, 0)

    def carry_copy(s, src):
        return pltpu.make_async_remote_copy(
            src_ref=src,
            dst_ref=cin.at[w],
            send_sem=car_send.at[s],
            recv_sem=car_recv.at[W - s],
            device_id={"wall": lax.rem(w + s, W)},
            device_id_type=pl.DeviceIdType.MESH,
        )

    for s in range(1, W):

        @pl.when(w + s < W)
        def _():
            carry_copy(s, fsend).start()

        @pl.when(w + s >= W)
        def _():
            carry_copy(s, esend).start()

    def solve(i, carry):
        n = lax.div(i, ncomp)
        c = lax.rem(i, ncomp)
        later = jnp.zeros((nx, nz), jnp.float32)
        for y in range(rows - 1, -1, -1):
            later = tab_p[y] * loc[n, c, y] + tab_rho[y] * later
            loc[n, c, y] = later
        return carry

    lax.fori_loop(0, fields, solve, 0)

    for s in range(1, W):
        pltpu.make_async_copy(fsend, cin.at[lax.rem(w + s, W)], car_recv.at[s]).wait()

    def finish(i, carry):
        n = lax.div(i, ncomp)
        c = lax.rem(i, ncomp)

        def forward(j, total):
            tile = ctiles[j]
            new = cin[j, n, c].astype(jnp.float32) + widen(tile[0]) * total
            return jnp.where(j < w, new, total)

        def backward(m, total):
            j = W - 1 - m
            tile = ctiles[j]
            new = cin[j, n, c].astype(jnp.float32) + widen(tile[1]) * total
            return jnp.where(j > w, new, total)

        zero = jnp.zeros((nx, nz), jnp.float32)
        f_in = lax.fori_loop(0, W - 1, forward, zero)
        b_in = lax.fori_loop(0, W - 1, backward, zero)
        b_in = b_in + tail * (fcar[n, c] + phi * f_in)
        for y in range(rows):
            adv_v[n, c, y] = loc[n, c, y] + tab_a[y] * f_in + tab_c[y] * b_in
        pltpu.make_async_copy(adv_v.at[n, c], adv_hbm.at[n, c], out_sem.at[i]).start()
        return carry

    lax.fori_loop(0, fields, finish, 0)

    @pl.when(w < W - 1)
    def _():
        halo_up().wait_send()

    @pl.when(w > 0)
    def _():
        halo_down().wait_send()

    def drain(k, carry):
        @pl.when(v < V - 1)
        def _():
            right_copy(k).wait_send()

        @pl.when(v > 0)
        def _():
            left_copy(k).wait_send()

        return carry

    lax.fori_loop(0, chunks, drain, 0)
    for s in range(1, W):
        coef_copy(s).wait_send()
        carry_copy(s, fsend).wait_send()

    def drain_out(i, carry):
        n = lax.div(i, ncomp)
        c = lax.rem(i, ncomp)
        pltpu.make_async_copy(adv_v.at[n, c], adv_hbm.at[n, c], out_sem.at[i]).wait()
        return carry

    lax.fori_loop(0, fields, drain_out, 0)
    advec_out.wait()


def on_device(W, V, q, prev, bs, step, slots, shift, gap, piv, up):
    nvec, ncomp, rows, nx, nz = q.shape
    chunks = rows // CHUNK_ROWS
    field = (nvec, ncomp, rows, nx, nz)
    slab = (ncomp, rows, nx, nz)
    edge = (nvec, ncomp, nx, nz)
    any_spec = pl.BlockSpec(memory_space=pl.ANY)
    smem = pl.BlockSpec(memory_space=pltpu.SMEM)
    f32, bf16 = jnp.float32, jnp.bfloat16
    dma = pltpu.SemaphoreType.DMA
    return pl.pallas_call(
        functools.partial(kernel, W, V),
        out_shape=(jax.ShapeDtypeStruct(field, f32), jax.ShapeDtypeStruct(field, bf16)),
        in_specs=[any_spec] * 3 + [smem] * 6,
        out_specs=(any_spec, any_spec),
        scratch_shapes=[
            pltpu.VMEM((nvec, ncomp, rows + 2, nx, nz), f32),
            pltpu.VMEM(field, bf16),
            pltpu.VMEM(bs.shape, bf16),
            pltpu.VMEM(slab, bf16),
            pltpu.VMEM(slab, bf16),
            pltpu.VMEM(slab, bf16),
            pltpu.VMEM(slab, bf16),
            pltpu.VMEM(field, f32),
            pltpu.VMEM(field, bf16),
            pltpu.VMEM(field, f32),
            pltpu.VMEM(edge, f32),
            pltpu.VMEM(edge, f32),
            pltpu.VMEM(edge, bf16),
            pltpu.VMEM(edge, bf16),
            pltpu.VMEM((W,) + edge, bf16),
            pltpu.VMEM((3, nx, 128), f32),
            pltpu.VMEM((W, 3, nx, 128), f32),
        ]
        + [pltpu.VMEM((rows, nx, nz), f32)] * 6
        + [
            dma((3,)),
            dma((2,)),
            dma((2,)),
            dma((W,)),
            dma((W,)),
            dma((chunks,)),
            dma((chunks,)),
            dma((chunks,)),
            dma((chunks,)),
            dma((W,)),
            dma((W,)),
            dma((nvec * ncomp + 1,)),
        ],
        compiler_params=pltpu.CompilerParams(
            collective_id=0, has_side_effects=True, vmem_limit_bytes=48 * 1024 * 1024
        ),
    )(q, prev, bs, step, slots, shift, gap, piv, up)


def solution(mesh):
    W, V = mesh.shape["wall"], mesh.shape["vec"]
    field = P("vec", None, "wall", None, None)
    return jax.shard_map(
        functools.partial(on_device, W, V),
        mesh=mesh,
        in_specs=(field, field, field, P(), P(), P(), P("wall"), P("wall"), P("wall")),
        out_specs=(field, field),
        check_vma=False,
    )
```

```python
import functools

import jax
import jax.numpy as jnp
from jax import lax
from jax.experimental import pallas as pl
from jax.experimental.pallas import tpu as pltpu
from jax.sharding import PartitionSpec as P

STEP_SIZE = 0.5
NEW_WEIGHT = 5.0 / 12.0
OLD_WEIGHT = -17.0 / 60.0
VISCOUS_WEIGHT = -0.06
CHUNK_ROWS = 2
HOP_LAG = 2


def kernel(
    W,
    V,
    q_hbm,
    prev_hbm,
    bs_hbm,
    step_h,
    slots_h,
    shift_h,
    gap_h,
    piv_h,
    up_h,
    adv_hbm,
    advec_hbm,
    step_s,
    slots_s,
    shift_s,
    gap_s,
    piv_s,
    up_s,
    dx_v,
    dy_v,
    dz_v,
    own_v,
    tab_f,
    tab_b,
    qpad,
    prev_v,
    bs_v,
    from_l,
    from_r,
    out_r,
    out_l,
    loc,
    expl,
    adv_v,
    fcar,
    bcar,
    fsend,
    esend,
    cin,
    ctile,
    ctiles,
    tab_d,
    tab_w,
    tab_p,
    tab_rho,
    tab_a,
    tab_c,
    in_sem,
    small_sem,
    halo_send,
    halo_recv,
    coef_send,
    coef_recv,
    lr_send,
    lr_recv,
    rl_send,
    rl_recv,
    car_send,
    car_recv,
    out_sem,
):
    w = lax.axis_index("wall")
    v = lax.axis_index("vec")
    nvec, ncomp, rows, nx, nz = q_hbm.shape
    stored = bs_hbm.shape[0]
    fields = nvec * ncomp
    chunks = rows // CHUNK_ROWS

    q_in = pltpu.make_async_copy(q_hbm, qpad.at[:, :, pl.ds(1, rows)], in_sem.at[0])
    prev_in = pltpu.make_async_copy(prev_hbm, prev_v, in_sem.at[1])
    bs_in = pltpu.make_async_copy(bs_hbm, bs_v, in_sem.at[2])
    small = [
        pltpu.make_async_copy(src, dst, small_sem.at[n])
        for n, (src, dst) in enumerate(
            (
                (step_h, step_s),
                (slots_h, slots_s),
                (shift_h, shift_s),
                (gap_h, gap_s),
                (piv_h, piv_s),
                (up_h, up_s),
            )
        )
    ]
    for copy in small:
        copy.start()
    bs_in.start()
    q_in.start()
    prev_in.start()

    barrier = pltpu.get_barrier_semaphore()
    for s in range(1, W):
        pl.semaphore_signal(
            barrier,
            inc=1,
            device_id={"wall": lax.rem(w + s, W)},
            device_id_type=pl.DeviceIdType.MESH,
        )

    @pl.when(v > 0)
    def _():
        pl.semaphore_signal(
            barrier, inc=1, device_id={"vec": v - 1}, device_id_type=pl.DeviceIdType.MESH
        )

    @pl.when(v < V - 1)
    def _():
        pl.semaphore_signal(
            barrier, inc=1, device_id={"vec": v + 1}, device_id_type=pl.DeviceIdType.MESH
        )

    @pl.when(w == 0)
    def _():
        qpad[:, :, 0] = jnp.zeros((nvec, ncomp, nx, nz), jnp.float32)

    @pl.when(w == W - 1)
    def _():
        qpad[:, :, rows + 1] = jnp.zeros((nvec, ncomp, nx, nz), jnp.float32)

    for copy in small:
        copy.wait()

    one = jnp.ones((nx, nz), jnp.float32)

    def down_tables(r, carry):
        prod_d, prod_rho, beta = carry
        d = 1.0 - gap_s[r]
        p = 1.0 / (one * piv_s[r])
        rho = p * up_s[r]
        prod_d = prod_d * d
        weight = prod_rho * p
        tab_d[r] = prod_d
        tab_w[r] = weight
        tab_p[r] = p
        tab_rho[r] = rho
        return prod_d, prod_rho * rho, beta + weight * prod_d

    phi, psi, beta = lax.fori_loop(0, rows, down_tables, (one, one, one * 0.0))
    ctile[0] = phi[:, :128]
    ctile[1] = psi[:, :128]
    ctile[2] = beta[:, :128]

    def up_tables(t, carry):
        a, c = carry
        r = rows - 1 - t
        a = tab_p[r] * tab_d[r] + tab_rho[r] * a
        c = tab_rho[r] * c
        tab_a[r] = a
        tab_c[r] = c
        return a, c

    lax.fori_loop(0, rows, up_tables, (one * 0.0, one))

    neighbours = jnp.where(v > 0, 1, 0) + jnp.where(v < V - 1, 1, 0)
    pl.semaphore_wait(barrier, W - 1 + neighbours)

    def halo_up():
        return pltpu.make_async_remote_copy(
            src_ref=q_hbm.at[:, :, rows - 1],
            dst_ref=qpad.at[:, :, 0],
            send_sem=halo_send.at[0],
            recv_sem=halo_recv.at[0],
            device_id={"wall": w + 1},
            device_id_type=pl.DeviceIdType.MESH,
        )

    def halo_down():
        return pltpu.make_async_remote_copy(
            src_ref=q_hbm.at[:, :, 0],
            dst_ref=qpad.at[:, :, rows + 1],
            send_sem=halo_send.at[1],
            recv_sem=halo_recv.at[1],
            device_id={"wall": w - 1},
            device_id_type=pl.DeviceIdType.MESH,
        )

    def right_copy(k, src):
        part = pl.ds(k * CHUNK_ROWS, CHUNK_ROWS)
        return pltpu.make_async_remote_copy(
            src_ref=src.at[:, part],
            dst_ref=from_l.at[:, part],
            send_sem=lr_send.at[k],
            recv_sem=lr_recv.at[k],
            device_id={"vec": v + 1},
            device_id_type=pl.DeviceIdType.MESH,
        )

    def left_copy(k, src):
        part = pl.ds(k * CHUNK_ROWS, CHUNK_ROWS)
        return pltpu.make_async_remote_copy(
            src_ref=src.at[:, part],
            dst_ref=from_r.at[:, part],
            send_sem=rl_send.at[k],
            recv_sem=rl_recv.at[k],
            device_id={"vec": v - 1},
            device_id_type=pl.DeviceIdType.MESH,
        )

    def coef_copy(s):
        peer = lax.rem(w + s, W)
        return pltpu.make_async_remote_copy(
            src_ref=ctile,
            dst_ref=ctiles.at[w],
            send_sem=coef_send.at[s],
            recv_sem=coef_recv.at[W - s],
            device_id={"wall": peer},
            device_id_type=pl.DeviceIdType.MESH,
        )

    def coef_wait(s):
        pltpu.make_async_copy(ctile, ctiles.at[lax.rem(w + s, W)], coef_recv.at[s]).wait()

    slot = slots_s[lax.rem(step_s[0], slots_s.shape[0])]
    owner = lax.div(slot, stored)
    local = lax.rem(slot, stored)
    mine = owner == v
    before = owner < v
    shift = shift_s[0]

    def own_row(c, y):
        value = bs_v[0, c, y]
        for s in range(1, stored):
            value = jnp.where(local == s, bs_v[s, c, y], value)
        return value

    @pl.when(w < W - 1)
    def _():
        halo_up().start()

    @pl.when(w > 0)
    def _():
        halo_down().start()

    bs_in.wait()

    def each_row(k, body):
        for m in range(CHUNK_ROWS):
            for c in range(ncomp):
                body(c, k * CHUNK_ROWS + m)

    def shift_own(k, carry):
        def put(c, y):
            row = pltpu.roll(own_row(c, y).astype(jnp.float32), shift, 1)
            own_v[c, y] = row.astype(jnp.bfloat16)

        each_row(k, put)

        @pl.when(v == 0)
        def _():
            right_copy(k, own_v).start()

        @pl.when(v == V - 1)
        def _():
            left_copy(k, own_v).start()

        return carry

    lax.fori_loop(0, chunks, shift_own, 0)

    for s in range(1, W):
        coef_copy(s).start()

    q_in.wait()
    prev_in.wait()

    def prepare(n, c, y):
        mid = qpad[n, c, y + 1]
        above = qpad[n, c, y + 2]
        below = qpad[n, c, y]
        dx_v[n, c, y] = 0.5 * (pltpu.roll(mid, nx - 1, 0) - pltpu.roll(mid, 1, 0))
        dz_v[n, c, y] = 0.5 * (pltpu.roll(mid, nz - 1, 1) - pltpu.roll(mid, 1, 1))
        dy_v[n, c, y] = 0.5 * (above - below)
        loc[n, c, y] = (
            mid
            + (STEP_SIZE * OLD_WEIGHT) * prev_v[n, c, y].astype(jnp.float32)
            + VISCOUS_WEIGHT * (above - 2.0 * mid + below)
        )

    def prepare_inner(i, carry):
        for y in range(1, rows - 1):
            prepare(lax.div(i, ncomp), lax.rem(i, ncomp), y)
        return carry

    def prepare_edges(i, carry):
        for y in (0, rows - 1):
            prepare(lax.div(i, ncomp), lax.rem(i, ncomp), y)
        return carry

    lax.fori_loop(0, fields, prepare_inner, 0)

    @pl.when(w < W - 1)
    def _():
        halo_down().wait_recv()

    @pl.when(w > 0)
    def _():
        halo_up().wait_recv()

    lax.fori_loop(0, fields, prepare_edges, 0)

    fcar[...] = jnp.zeros_like(fcar)
    bcar[...] = jnp.zeros_like(bcar)

    def compute_chunk(k):
        for m in range(CHUNK_ROWS):
            y = k * CHUNK_ROWS + m
            base = []
            for c in range(ncomp):
                got = jnp.where(before, from_l[c, y], from_r[c, y])
                base.append(jnp.where(mine, own_v[c, y], got).astype(jnp.float32))
            d = 1.0 - gap_s[y]
            weight = tab_w[y]
            for n in range(nvec):
                for c in range(ncomp):
                    explicit = -(
                        base[0] * dx_v[n, c, y] + base[1] * dy_v[n, c, y] + base[2] * dz_v[n, c, y]
                    )
                    expl[n, c, y] = explicit.astype(jnp.bfloat16)
                    source = loc[n, c, y] + (STEP_SIZE * NEW_WEIGHT) * explicit
                    swept = source + d * fcar[n, c]
                    fcar[n, c] = swept
                    bcar[n, c] = bcar[n, c] + weight * swept
                    loc[n, c, y] = swept

    far = V - 1 - v

    def slot_step(t, carry):
        kl = t - HOP_LAG * v
        kr = t - HOP_LAG * far

        @pl.when((v > 0) & (kl >= 0) & (kl < chunks))
        def _():
            right_copy(kl, own_v).wait_recv()

            @pl.when(v < V - 1)
            def _():
                def put(c, y):
                    out_r[c, y] = jnp.where(mine, own_v[c, y], from_l[c, y])

                each_row(kl, put)
                right_copy(kl, out_r).start()

        @pl.when((v < V - 1) & (kr >= 0) & (kr < chunks))
        def _():
            left_copy(kr, own_v).wait_recv()

            @pl.when(v > 0)
            def _():
                def put(c, y):
                    out_l[c, y] = jnp.where(mine, own_v[c, y], from_r[c, y])

                each_row(kr, put)
                left_copy(kr, out_l).start()

        kc = jnp.minimum(kl, kr)

        @pl.when((kc >= 0) & (kc < chunks))
        def _():
            compute_chunk(kc)

        return carry

    lax.fori_loop(0, chunks + HOP_LAG * (V - 1), slot_step, 0)

    advec_out = pltpu.make_async_copy(expl, advec_hbm, out_sem.at[fields])
    advec_out.start()

    for s in range(1, W):
        coef_wait(s)

    def tail_response(m, total):
        j = W - 1 - m
        tile = ctiles[j]
        new = tile[2] + tile[1] * total * tile[0]
        return jnp.where(j > w, new, total)

    wide = nz // 128

    def widen(x):
        return jnp.concatenate([x] * wide, axis=-1)

    tail = widen(lax.fori_loop(0, W - 1, tail_response, jnp.zeros((nx, 128), jnp.float32)))
    gain = psi * tail

    for n in range(nvec):
        for c in range(ncomp):
            f = fcar[n, c]
            fsend[n, c] = f.astype(jnp.bfloat16)
            esend[n, c] = (bcar[n, c] + gain * f).astype(jnp.bfloat16)

    def carry_copy(s, src):
        return pltpu.make_async_remote_copy(
            src_ref=src,
            dst_ref=cin.at[w],
            send_sem=car_send.at[s],
            recv_sem=car_recv.at[W - s],
            device_id={"wall": lax.rem(w + s, W)},
            device_id_type=pl.DeviceIdType.MESH,
        )

    for s in range(1, W):

        @pl.when(w + s < W)
        def _():
            carry_copy(s, fsend).start()

        @pl.when(w + s >= W)
        def _():
            carry_copy(s, esend).start()

    def solve(i, carry):
        n = lax.div(i, ncomp)
        c = lax.rem(i, ncomp)
        later = jnp.zeros((nx, nz), jnp.float32)
        for y in range(rows - 1, -1, -1):
            later = tab_p[y] * loc[n, c, y] + tab_rho[y] * later
            loc[n, c, y] = later
        return carry

    lax.fori_loop(0, fields, solve, 0)

    def forward_weight(m, prod):
        j = w - 1 - m
        tab_f[j] = prod
        return prod * widen(ctiles[j, 0])

    def backward_weight(m, prod):
        j = w + 1 + m
        tab_b[j] = prod
        return prod * widen(ctiles[j, 1])

    tab_f[...] = jnp.zeros_like(tab_f)
    tab_b[...] = jnp.zeros_like(tab_b)
    lax.fori_loop(0, w, forward_weight, one)
    lax.fori_loop(0, W - 1 - w, backward_weight, one)

    pairs = [(n, c) for n in range(nvec) for c in range(ncomp)]

    def gather(s, sums):
        j = lax.rem(w + s, W)
        pltpu.make_async_copy(fsend, cin.at[j], car_recv.at[s]).wait()
        wf, wb = tab_f[j], tab_b[j]
        new = []
        for (n, c), (f_in, b_in) in zip(pairs, sums):
            value = cin[j, n, c].astype(jnp.float32)
            new.append((f_in + wf * value, b_in + wb * value))
        return tuple(new)

    sums = tuple((one * 0.0, one * 0.0) for _ in pairs)
    sums = lax.fori_loop(1, W, gather, sums)
    for (n, c), (f_in, b_in) in zip(pairs, sums):
        bcar[n, c] = b_in + tail * (fcar[n, c] + phi * f_in)
        fcar[n, c] = f_in

    def finish(i, carry):
        n = lax.div(i, ncomp)
        c = lax.rem(i, ncomp)
        f_in = fcar[n, c]
        b_in = bcar[n, c]
        for y in range(rows):
            adv_v[n, c, y] = loc[n, c, y] + tab_a[y] * f_in + tab_c[y] * b_in
        pltpu.make_async_copy(adv_v.at[n, c], adv_hbm.at[n, c], out_sem.at[i]).start()
        return carry

    lax.fori_loop(0, fields, finish, 0)

    @pl.when(w < W - 1)
    def _():
        halo_up().wait_send()

    @pl.when(w > 0)
    def _():
        halo_down().wait_send()

    def drain(k, carry):
        @pl.when(v < V - 1)
        def _():
            right_copy(k, own_v).wait_send()

        @pl.when(v > 0)
        def _():
            left_copy(k, own_v).wait_send()

        return carry

    lax.fori_loop(0, chunks, drain, 0)
    for s in range(1, W):
        coef_copy(s).wait_send()
        carry_copy(s, fsend).wait_send()

    def drain_out(i, carry):
        n = lax.div(i, ncomp)
        c = lax.rem(i, ncomp)
        pltpu.make_async_copy(adv_v.at[n, c], adv_hbm.at[n, c], out_sem.at[i]).wait()
        return carry

    lax.fori_loop(0, fields, drain_out, 0)
    advec_out.wait()


def on_device(W, V, q, prev, bs, step, slots, shift, gap, piv, up):
    nvec, ncomp, rows, nx, nz = q.shape
    chunks = rows // CHUNK_ROWS
    field = (nvec, ncomp, rows, nx, nz)
    slab = (ncomp, rows, nx, nz)
    edge = (nvec, ncomp, nx, nz)
    any_spec = pl.BlockSpec(memory_space=pl.ANY)
    hbm = pl.BlockSpec(memory_space=pltpu.HBM)
    f32, bf16 = jnp.float32, jnp.bfloat16
    dma = pltpu.SemaphoreType.DMA
    return pl.pallas_call(
        functools.partial(kernel, W, V),
        out_shape=(jax.ShapeDtypeStruct(field, f32), jax.ShapeDtypeStruct(field, bf16)),
        in_specs=[hbm] * 9,
        out_specs=(any_spec, any_spec),
        scratch_shapes=[
            pltpu.SMEM(step.shape, step.dtype),
            pltpu.SMEM(slots.shape, slots.dtype),
            pltpu.SMEM(shift.shape, shift.dtype),
            pltpu.SMEM(gap.shape, gap.dtype),
            pltpu.SMEM(piv.shape, piv.dtype),
            pltpu.SMEM(up.shape, up.dtype),
            pltpu.VMEM(field, f32),
            pltpu.VMEM(field, f32),
            pltpu.VMEM(field, f32),
            pltpu.VMEM(slab, bf16),
            pltpu.VMEM((W, nx, nz), f32),
            pltpu.VMEM((W, nx, nz), f32),
            pltpu.VMEM((nvec, ncomp, rows + 2, nx, nz), f32),
            pltpu.VMEM(field, bf16),
            pltpu.VMEM(bs.shape, bf16),
            pltpu.VMEM(slab, bf16),
            pltpu.VMEM(slab, bf16),
            pltpu.VMEM(slab, bf16),
            pltpu.VMEM(slab, bf16),
            pltpu.VMEM(field, f32),
            pltpu.VMEM(field, bf16),
            pltpu.VMEM(field, f32),
            pltpu.VMEM(edge, f32),
            pltpu.VMEM(edge, f32),
            pltpu.VMEM(edge, bf16),
            pltpu.VMEM(edge, bf16),
            pltpu.VMEM((W,) + edge, bf16),
            pltpu.VMEM((3, nx, 128), f32),
            pltpu.VMEM((W, 3, nx, 128), f32),
        ]
        + [pltpu.VMEM((rows, nx, nz), f32)] * 6
        + [
            dma((3,)),
            dma((6,)),
            dma((2,)),
            dma((2,)),
            dma((W,)),
            dma((W,)),
            dma((chunks,)),
            dma((chunks,)),
            dma((chunks,)),
            dma((chunks,)),
            dma((W,)),
            dma((W,)),
            dma((nvec * ncomp + 1,)),
        ],
        compiler_params=pltpu.CompilerParams(
            collective_id=0, has_side_effects=True, vmem_limit_bytes=63 * 1024 * 1024
        ),
    )(q, prev, bs, step, slots, shift, gap, piv, up)


def solution(mesh):
    W, V = mesh.shape["wall"], mesh.shape["vec"]
    field = P("vec", None, "wall", None, None)
    return jax.shard_map(
        functools.partial(on_device, W, V),
        mesh=mesh,
        in_specs=(field, field, field, P(), P(), P(), P("wall"), P("wall"), P("wall")),
        out_specs=(field, field),
        check_vma=False,
    )
```

```python
import functools

import jax
import jax.numpy as jnp
from jax import lax
from jax.experimental import pallas as pl
from jax.experimental.pallas import tpu as pltpu
from jax.sharding import PartitionSpec as P

STEP_SIZE = 0.5
NEW_WEIGHT = 5.0 / 12.0
OLD_WEIGHT = -17.0 / 60.0
VISCOUS_WEIGHT = -0.06
CHUNK_ROWS = 2
HOP_LAG = 3
PREP_UNROLL = 2


def kernel(
    W,
    V,
    q_hbm,
    prev_hbm,
    bs_hbm,
    step_h,
    slots_h,
    shift_h,
    gap_h,
    piv_h,
    up_h,
    adv_hbm,
    advec_hbm,
    step_s,
    slots_s,
    shift_s,
    gap_s,
    piv_s,
    up_s,
    dx_v,
    dy_v,
    dz_v,
    own_v,
    tab_f,
    tab_b,
    qpad,
    prev_v,
    bs_v,
    from_l,
    from_r,
    out_r,
    out_l,
    loc,
    expl,
    adv_v,
    fcar,
    bcar,
    fsend,
    esend,
    cin,
    ctile,
    ctiles,
    tab_d,
    tab_w,
    tab_p,
    tab_rho,
    tab_a,
    tab_c,
    in_sem,
    small_sem,
    halo_send,
    halo_recv,
    coef_send,
    coef_recv,
    lr_send,
    lr_recv,
    rl_send,
    rl_recv,
    car_send,
    car_recv,
    out_sem,
):
    w = lax.axis_index("wall")
    v = lax.axis_index("vec")
    nvec, ncomp, rows, nx, nz = q_hbm.shape
    stored = bs_hbm.shape[0]
    fields = nvec * ncomp
    chunks = rows // CHUNK_ROWS

    q_in = pltpu.make_async_copy(q_hbm, qpad.at[:, :, pl.ds(1, rows)], in_sem.at[0])
    prev_in = pltpu.make_async_copy(prev_hbm, prev_v, in_sem.at[1])
    bs_in = pltpu.make_async_copy(bs_hbm, bs_v, in_sem.at[2])
    small = [
        pltpu.make_async_copy(src, dst, small_sem.at[n])
        for n, (src, dst) in enumerate(
            (
                (step_h, step_s),
                (slots_h, slots_s),
                (shift_h, shift_s),
                (gap_h, gap_s),
                (piv_h, piv_s),
                (up_h, up_s),
            )
        )
    ]
    for copy in small:
        copy.start()
    bs_in.start()
    q_in.start()
    prev_in.start()

    barrier = pltpu.get_barrier_semaphore()
    for s in range(1, W):
        pl.semaphore_signal(
            barrier,
            inc=1,
            device_id={"wall": lax.rem(w + s, W)},
            device_id_type=pl.DeviceIdType.MESH,
        )

    @pl.when(v > 0)
    def _():
        pl.semaphore_signal(
            barrier, inc=1, device_id={"vec": v - 1}, device_id_type=pl.DeviceIdType.MESH
        )

    @pl.when(v < V - 1)
    def _():
        pl.semaphore_signal(
            barrier, inc=1, device_id={"vec": v + 1}, device_id_type=pl.DeviceIdType.MESH
        )

    @pl.when(w == 0)
    def _():
        qpad[:, :, 0] = jnp.zeros((nvec, ncomp, nx, nz), jnp.float32)

    @pl.when(w == W - 1)
    def _():
        qpad[:, :, rows + 1] = jnp.zeros((nvec, ncomp, nx, nz), jnp.float32)

    for copy in small:
        copy.wait()

    one = jnp.ones((nx, nz), jnp.float32)

    def down_tables(r, carry):
        prod_d, prod_rho, beta = carry
        d = 1.0 - gap_s[r]
        p = 1.0 / (one * piv_s[r])
        rho = p * up_s[r]
        prod_d = prod_d * d
        weight = prod_rho * p
        tab_d[r] = prod_d
        tab_w[r] = weight
        tab_p[r] = p
        tab_rho[r] = rho
        return prod_d, prod_rho * rho, beta + weight * prod_d

    phi, psi, beta = lax.fori_loop(0, rows, down_tables, (one, one, one * 0.0))
    ctile[0] = phi[:, :128]
    ctile[1] = psi[:, :128]
    ctile[2] = beta[:, :128]

    def up_tables(t, carry):
        a, c = carry
        r = rows - 1 - t
        a = tab_p[r] * tab_d[r] + tab_rho[r] * a
        c = tab_rho[r] * c
        tab_a[r] = a
        tab_c[r] = c
        return a, c

    lax.fori_loop(0, rows, up_tables, (one * 0.0, one))

    neighbours = jnp.where(v > 0, 1, 0) + jnp.where(v < V - 1, 1, 0)
    pl.semaphore_wait(barrier, W - 1 + neighbours)

    def halo_up():
        return pltpu.make_async_remote_copy(
            src_ref=q_hbm.at[:, :, rows - 1],
            dst_ref=qpad.at[:, :, 0],
            send_sem=halo_send.at[0],
            recv_sem=halo_recv.at[0],
            device_id={"wall": w + 1},
            device_id_type=pl.DeviceIdType.MESH,
        )

    def halo_down():
        return pltpu.make_async_remote_copy(
            src_ref=q_hbm.at[:, :, 0],
            dst_ref=qpad.at[:, :, rows + 1],
            send_sem=halo_send.at[1],
            recv_sem=halo_recv.at[1],
            device_id={"wall": w - 1},
            device_id_type=pl.DeviceIdType.MESH,
        )

    def right_copy(k, src):
        part = pl.ds(k * CHUNK_ROWS, CHUNK_ROWS)
        return pltpu.make_async_remote_copy(
            src_ref=src.at[:, part],
            dst_ref=from_l.at[:, part],
            send_sem=lr_send.at[k],
            recv_sem=lr_recv.at[k],
            device_id={"vec": v + 1},
            device_id_type=pl.DeviceIdType.MESH,
        )

    def left_copy(k, src):
        part = pl.ds(k * CHUNK_ROWS, CHUNK_ROWS)
        return pltpu.make_async_remote_copy(
            src_ref=src.at[:, part],
            dst_ref=from_r.at[:, part],
            send_sem=rl_send.at[k],
            recv_sem=rl_recv.at[k],
            device_id={"vec": v - 1},
            device_id_type=pl.DeviceIdType.MESH,
        )

    def coef_copy(s):
        peer = lax.rem(w + s, W)
        return pltpu.make_async_remote_copy(
            src_ref=ctile,
            dst_ref=ctiles.at[w],
            send_sem=coef_send.at[s],
            recv_sem=coef_recv.at[W - s],
            device_id={"wall": peer},
            device_id_type=pl.DeviceIdType.MESH,
        )

    def coef_wait(s):
        pltpu.make_async_copy(ctile, ctiles.at[lax.rem(w + s, W)], coef_recv.at[s]).wait()

    slot = slots_s[lax.rem(step_s[0], slots_s.shape[0])]
    owner = lax.div(slot, stored)
    local = lax.rem(slot, stored)
    mine = owner == v
    before = owner < v
    shift = shift_s[0]

    def own_row(c, y):
        value = bs_v[0, c, y]
        for s in range(1, stored):
            value = jnp.where(local == s, bs_v[s, c, y], value)
        return value

    @pl.when(w < W - 1)
    def _():
        halo_up().start()

    @pl.when(w > 0)
    def _():
        halo_down().start()

    bs_in.wait()

    def each_row(k, body):
        for m in range(CHUNK_ROWS):
            for c in range(ncomp):
                body(c, k * CHUNK_ROWS + m)

    def shift_own(k, carry):
        def put(c, y):
            row = pltpu.roll(own_row(c, y).astype(jnp.float32), shift, 1)
            own_v[c, y] = row.astype(jnp.bfloat16)

        each_row(k, put)

        @pl.when(v == 0)
        def _():
            right_copy(k, own_v).start()

        @pl.when(v == V - 1)
        def _():
            left_copy(k, own_v).start()

        return carry

    lax.fori_loop(0, chunks, shift_own, 0)

    for s in range(1, W):
        coef_copy(s).start()

    q_in.wait()
    prev_in.wait()

    def prepare(n, c, y):
        mid = qpad[n, c, y + 1]
        above = qpad[n, c, y + 2]
        below = qpad[n, c, y]
        dx_v[n, c, y] = 0.5 * (pltpu.roll(mid, nx - 1, 0) - pltpu.roll(mid, 1, 0))
        dz_v[n, c, y] = 0.5 * (pltpu.roll(mid, nz - 1, 1) - pltpu.roll(mid, 1, 1))
        dy_v[n, c, y] = 0.5 * (above - below)
        loc[n, c, y] = (
            mid
            + (STEP_SIZE * OLD_WEIGHT) * prev_v[n, c, y].astype(jnp.float32)
            + VISCOUS_WEIGHT * (above - 2.0 * mid + below)
        )

    def prepare_chunk(p):
        def run(i, carry):
            for m in range(CHUNK_ROWS):
                prepare(lax.div(i, ncomp), lax.rem(i, ncomp), p * CHUNK_ROWS + m)
            return carry

        @pl.when((p == 0) & (w > 0))
        def _():
            halo_up().wait_recv()

        @pl.when((p == chunks - 1) & (w < W - 1))
        def _():
            halo_down().wait_recv()

        lax.fori_loop(0, fields, run, 0, unroll=PREP_UNROLL)

    fcar[...] = jnp.zeros_like(fcar)
    bcar[...] = jnp.zeros_like(bcar)

    def compute_chunk(k):
        for m in range(CHUNK_ROWS):
            y = k * CHUNK_ROWS + m
            base = []
            for c in range(ncomp):
                got = jnp.where(before, from_l[c, y], from_r[c, y])
                base.append(jnp.where(mine, own_v[c, y], got).astype(jnp.float32))
            d = 1.0 - gap_s[y]
            weight = tab_w[y]
            for n in range(nvec):
                for c in range(ncomp):
                    explicit = -(
                        base[0] * dx_v[n, c, y] + base[1] * dy_v[n, c, y] + base[2] * dz_v[n, c, y]
                    )
                    expl[n, c, y] = explicit.astype(jnp.bfloat16)
                    source = loc[n, c, y] + (STEP_SIZE * NEW_WEIGHT) * explicit
                    swept = source + d * fcar[n, c]
                    fcar[n, c] = swept
                    bcar[n, c] = bcar[n, c] + weight * swept
                    loc[n, c, y] = swept

    far = V - 1 - v

    def slot_step(t, carry):
        kl = t - HOP_LAG * v
        kr = t - HOP_LAG * far

        @pl.when((v > 0) & (kl >= 0) & (kl < chunks))
        def _():
            right_copy(kl, own_v).wait_recv()

            @pl.when(v < V - 1)
            def _():
                def put(c, y):
                    out_r[c, y] = jnp.where(mine, own_v[c, y], from_l[c, y])

                each_row(kl, put)
                right_copy(kl, out_r).start()

        @pl.when((v < V - 1) & (kr >= 0) & (kr < chunks))
        def _():
            left_copy(kr, own_v).wait_recv()

            @pl.when(v > 0)
            def _():
                def put(c, y):
                    out_l[c, y] = jnp.where(mine, own_v[c, y], from_r[c, y])

                each_row(kr, put)
                left_copy(kr, out_l).start()

        @pl.when(t < chunks)
        def _():
            prepare_chunk(jnp.where(t < 2, t + 1, jnp.where(t == 2, 0, t)))

        kc = jnp.minimum(kl, kr)

        @pl.when((kc >= 0) & (kc < chunks))
        def _():
            compute_chunk(kc)

        return carry

    lax.fori_loop(0, chunks + HOP_LAG * (V - 1), slot_step, 0)

    advec_out = pltpu.make_async_copy(expl, advec_hbm, out_sem.at[fields])
    advec_out.start()

    for s in range(1, W):
        coef_wait(s)

    def tail_response(m, total):
        j = W - 1 - m
        tile = ctiles[j]
        new = tile[2] + tile[1] * total * tile[0]
        return jnp.where(j > w, new, total)

    wide = nz // 128

    def widen(x):
        return jnp.concatenate([x] * wide, axis=-1)

    tail = widen(lax.fori_loop(0, W - 1, tail_response, jnp.zeros((nx, 128), jnp.float32)))
    gain = psi * tail

    for n in range(nvec):
        for c in range(ncomp):
            f = fcar[n, c]
            fsend[n, c] = f.astype(jnp.bfloat16)
            esend[n, c] = (bcar[n, c] + gain * f).astype(jnp.bfloat16)

    def carry_copy(s, src):
        return pltpu.make_async_remote_copy(
            src_ref=src,
            dst_ref=cin.at[w],
            send_sem=car_send.at[s],
            recv_sem=car_recv.at[W - s],
            device_id={"wall": lax.rem(w + s, W)},
            device_id_type=pl.DeviceIdType.MESH,
        )

    for s in range(1, W):

        @pl.when(w + s < W)
        def _():
            carry_copy(s, fsend).start()

        @pl.when(w + s >= W)
        def _():
            carry_copy(s, esend).start()

    def solve(i, carry):
        n = lax.div(i, ncomp)
        c = lax.rem(i, ncomp)
        later = jnp.zeros((nx, nz), jnp.float32)
        for y in range(rows - 1, -1, -1):
            later = tab_p[y] * loc[n, c, y] + tab_rho[y] * later
            loc[n, c, y] = later
        return carry

    lax.fori_loop(0, fields, solve, 0)

    def forward_weight(m, prod):
        j = w - 1 - m
        tab_f[j] = prod
        return prod * widen(ctiles[j, 0])

    def backward_weight(m, prod):
        j = w + 1 + m
        tab_b[j] = prod
        return prod * widen(ctiles[j, 1])

    tab_f[...] = jnp.zeros_like(tab_f)
    tab_b[...] = jnp.zeros_like(tab_b)
    lax.fori_loop(0, w, forward_weight, one)
    lax.fori_loop(0, W - 1 - w, backward_weight, one)

    pairs = [(n, c) for n in range(nvec) for c in range(ncomp)]

    def gather(s, sums):
        j = lax.rem(w + s, W)
        pltpu.make_async_copy(fsend, cin.at[j], car_recv.at[s]).wait()
        wf, wb = tab_f[j], tab_b[j]
        new = []
        for (n, c), (f_in, b_in) in zip(pairs, sums):
            value = cin[j, n, c].astype(jnp.float32)
            new.append((f_in + wf * value, b_in + wb * value))
        return tuple(new)

    sums = tuple((one * 0.0, one * 0.0) for _ in pairs)
    sums = lax.fori_loop(1, W, gather, sums)
    for (n, c), (f_in, b_in) in zip(pairs, sums):
        bcar[n, c] = b_in + tail * (fcar[n, c] + phi * f_in)
        fcar[n, c] = f_in

    def finish(i, carry):
        n = lax.div(i, ncomp)
        c = lax.rem(i, ncomp)
        f_in = fcar[n, c]
        b_in = bcar[n, c]
        for y in range(rows):
            adv_v[n, c, y] = loc[n, c, y] + tab_a[y] * f_in + tab_c[y] * b_in
        pltpu.make_async_copy(adv_v.at[n, c], adv_hbm.at[n, c], out_sem.at[i]).start()
        return carry

    lax.fori_loop(0, fields, finish, 0)

    @pl.when(w < W - 1)
    def _():
        halo_up().wait_send()

    @pl.when(w > 0)
    def _():
        halo_down().wait_send()

    def drain(k, carry):
        @pl.when(v < V - 1)
        def _():
            right_copy(k, own_v).wait_send()

        @pl.when(v > 0)
        def _():
            left_copy(k, own_v).wait_send()

        return carry

    lax.fori_loop(0, chunks, drain, 0)
    for s in range(1, W):
        coef_copy(s).wait_send()
        carry_copy(s, fsend).wait_send()

    def drain_out(i, carry):
        n = lax.div(i, ncomp)
        c = lax.rem(i, ncomp)
        pltpu.make_async_copy(adv_v.at[n, c], adv_hbm.at[n, c], out_sem.at[i]).wait()
        return carry

    lax.fori_loop(0, fields, drain_out, 0)
    advec_out.wait()


def on_device(W, V, q, prev, bs, step, slots, shift, gap, piv, up):
    nvec, ncomp, rows, nx, nz = q.shape
    chunks = rows // CHUNK_ROWS
    field = (nvec, ncomp, rows, nx, nz)
    slab = (ncomp, rows, nx, nz)
    edge = (nvec, ncomp, nx, nz)
    any_spec = pl.BlockSpec(memory_space=pl.ANY)
    hbm = pl.BlockSpec(memory_space=pltpu.HBM)
    f32, bf16 = jnp.float32, jnp.bfloat16
    dma = pltpu.SemaphoreType.DMA
    return pl.pallas_call(
        functools.partial(kernel, W, V),
        out_shape=(jax.ShapeDtypeStruct(field, f32), jax.ShapeDtypeStruct(field, bf16)),
        in_specs=[hbm] * 9,
        out_specs=(any_spec, any_spec),
        scratch_shapes=[
            pltpu.SMEM(step.shape, step.dtype),
            pltpu.SMEM(slots.shape, slots.dtype),
            pltpu.SMEM(shift.shape, shift.dtype),
            pltpu.SMEM(gap.shape, gap.dtype),
            pltpu.SMEM(piv.shape, piv.dtype),
            pltpu.SMEM(up.shape, up.dtype),
            pltpu.VMEM(field, f32),
            pltpu.VMEM(field, f32),
            pltpu.VMEM(field, f32),
            pltpu.VMEM(slab, bf16),
            pltpu.VMEM((W, nx, nz), f32),
            pltpu.VMEM((W, nx, nz), f32),
            pltpu.VMEM((nvec, ncomp, rows + 2, nx, nz), f32),
            pltpu.VMEM(field, bf16),
            pltpu.VMEM(bs.shape, bf16),
            pltpu.VMEM(slab, bf16),
            pltpu.VMEM(slab, bf16),
            pltpu.VMEM(slab, bf16),
            pltpu.VMEM(slab, bf16),
            pltpu.VMEM(field, f32),
            pltpu.VMEM(field, bf16),
            pltpu.VMEM(field, f32),
            pltpu.VMEM(edge, f32),
            pltpu.VMEM(edge, f32),
            pltpu.VMEM(edge, bf16),
            pltpu.VMEM(edge, bf16),
            pltpu.VMEM((W,) + edge, bf16),
            pltpu.VMEM((3, nx, 128), f32),
            pltpu.VMEM((W, 3, nx, 128), f32),
        ]
        + [pltpu.VMEM((rows, nx, nz), f32)] * 6
        + [
            dma((3,)),
            dma((6,)),
            dma((2,)),
            dma((2,)),
            dma((W,)),
            dma((W,)),
            dma((chunks,)),
            dma((chunks,)),
            dma((chunks,)),
            dma((chunks,)),
            dma((W,)),
            dma((W,)),
            dma((nvec * ncomp + 1,)),
        ],
        compiler_params=pltpu.CompilerParams(
            collective_id=0, has_side_effects=True, vmem_limit_bytes=63 * 1024 * 1024
        ),
    )(q, prev, bs, step, slots, shift, gap, piv, up)


def solution(mesh):
    W, V = mesh.shape["wall"], mesh.shape["vec"]
    field = P("vec", None, "wall", None, None)
    return jax.shard_map(
        functools.partial(on_device, W, V),
        mesh=mesh,
        in_specs=(field, field, field, P(), P(), P(), P("wall"), P("wall"), P("wall")),
        out_specs=(field, field),
        check_vma=False,
    )
```

```python
import functools

import jax
import jax.numpy as jnp
from jax import lax
from jax.experimental import pallas as pl
from jax.experimental.pallas import tpu as pltpu
from jax.sharding import PartitionSpec as P

STEP_SIZE = 0.5
NEW_WEIGHT = 5.0 / 12.0
OLD_WEIGHT = -17.0 / 60.0
VISCOUS_WEIGHT = -0.06
CHUNK_ROWS = 2
HOP_LAG = 3
PREP_UNROLL = 2


def kernel(
    W,
    V,
    q_hbm,
    prev_hbm,
    bs_hbm,
    step_h,
    slots_h,
    shift_h,
    gap_h,
    piv_h,
    up_h,
    part_hbm,
    advec_hbm,
    f_hbm,
    b_hbm,
    a_hbm,
    c_hbm,
    step_s,
    slots_s,
    shift_s,
    gap_s,
    piv_s,
    up_s,
    dx_v,
    dy_v,
    dz_v,
    own_v,
    tab_f,
    tab_b,
    qpad,
    prev_v,
    bs_v,
    from_l,
    from_r,
    out_r,
    out_l,
    loc,
    expl,
    edges,
    fcar,
    bcar,
    fsend,
    esend,
    cin,
    ctile,
    ctiles,
    tab_d,
    tab_w,
    tab_p,
    tab_rho,
    tabs,
    in_sem,
    small_sem,
    halo_send,
    halo_recv,
    coef_send,
    coef_recv,
    lr_send,
    lr_recv,
    rl_send,
    rl_recv,
    car_send,
    car_recv,
    out_sem,
):
    w = lax.axis_index("wall")
    v = lax.axis_index("vec")
    nvec, ncomp, rows, nx, nz = q_hbm.shape
    stored = bs_hbm.shape[0]
    fields = nvec * ncomp
    chunks = rows // CHUNK_ROWS

    q_in = pltpu.make_async_copy(q_hbm, qpad.at[:, :, pl.ds(1, rows)], in_sem.at[0])
    prev_in = pltpu.make_async_copy(prev_hbm, prev_v, in_sem.at[1])
    bs_in = pltpu.make_async_copy(bs_hbm, bs_v, in_sem.at[2])
    small = [
        pltpu.make_async_copy(src, dst, small_sem.at[n])
        for n, (src, dst) in enumerate(
            (
                (step_h, step_s),
                (slots_h, slots_s),
                (shift_h, shift_s),
                (gap_h, gap_s),
                (piv_h, piv_s),
                (up_h, up_s),
            )
        )
    ]
    for copy in small:
        copy.start()
    bs_in.start()
    q_in.start()
    prev_in.start()

    barrier = pltpu.get_barrier_semaphore()
    for s in range(1, W):
        pl.semaphore_signal(
            barrier,
            inc=1,
            device_id={"wall": lax.rem(w + s, W)},
            device_id_type=pl.DeviceIdType.MESH,
        )

    @pl.when(v > 0)
    def _():
        pl.semaphore_signal(
            barrier, inc=1, device_id={"vec": v - 1}, device_id_type=pl.DeviceIdType.MESH
        )

    @pl.when(v < V - 1)
    def _():
        pl.semaphore_signal(
            barrier, inc=1, device_id={"vec": v + 1}, device_id_type=pl.DeviceIdType.MESH
        )

    @pl.when(w == 0)
    def _():
        qpad[:, :, 0] = jnp.zeros((nvec, ncomp, nx, nz), jnp.float32)

    @pl.when(w == W - 1)
    def _():
        qpad[:, :, rows + 1] = jnp.zeros((nvec, ncomp, nx, nz), jnp.float32)

    for copy in small:
        copy.wait()

    one = jnp.ones((nx, nz), jnp.float32)

    def down_tables(r, carry):
        prod_d, prod_rho, beta = carry
        d = 1.0 - gap_s[r]
        p = 1.0 / (one * piv_s[r])
        rho = p * up_s[r]
        prod_d = prod_d * d
        weight = prod_rho * p
        tab_d[r] = prod_d
        tab_w[r] = weight
        tab_p[r] = p
        tab_rho[r] = rho
        return prod_d, prod_rho * rho, beta + weight * prod_d

    phi, psi, beta = lax.fori_loop(0, rows, down_tables, (one, one, one * 0.0))
    ctile[0] = phi[:, :128]
    ctile[1] = psi[:, :128]
    ctile[2] = beta[:, :128]

    def up_tables(t, carry):
        a, c = carry
        r = rows - 1 - t
        a = tab_p[r] * tab_d[r] + tab_rho[r] * a
        c = tab_rho[r] * c
        tabs[0, r] = a
        tabs[1, r] = c
        return a, c

    lax.fori_loop(0, rows, up_tables, (one * 0.0, one))

    neighbours = jnp.where(v > 0, 1, 0) + jnp.where(v < V - 1, 1, 0)
    pl.semaphore_wait(barrier, W - 1 + neighbours)

    def halo_up():
        return pltpu.make_async_remote_copy(
            src_ref=q_hbm.at[:, :, rows - 1],
            dst_ref=qpad.at[:, :, 0],
            send_sem=halo_send.at[0],
            recv_sem=halo_recv.at[0],
            device_id={"wall": w + 1},
            device_id_type=pl.DeviceIdType.MESH,
        )

    def halo_down():
        return pltpu.make_async_remote_copy(
            src_ref=q_hbm.at[:, :, 0],
            dst_ref=qpad.at[:, :, rows + 1],
            send_sem=halo_send.at[1],
            recv_sem=halo_recv.at[1],
            device_id={"wall": w - 1},
            device_id_type=pl.DeviceIdType.MESH,
        )

    def right_copy(k, src):
        part = pl.ds(k * CHUNK_ROWS, CHUNK_ROWS)
        return pltpu.make_async_remote_copy(
            src_ref=src.at[:, part],
            dst_ref=from_l.at[:, part],
            send_sem=lr_send.at[k],
            recv_sem=lr_recv.at[k],
            device_id={"vec": v + 1},
            device_id_type=pl.DeviceIdType.MESH,
        )

    def left_copy(k, src):
        part = pl.ds(k * CHUNK_ROWS, CHUNK_ROWS)
        return pltpu.make_async_remote_copy(
            src_ref=src.at[:, part],
            dst_ref=from_r.at[:, part],
            send_sem=rl_send.at[k],
            recv_sem=rl_recv.at[k],
            device_id={"vec": v - 1},
            device_id_type=pl.DeviceIdType.MESH,
        )

    def coef_copy(s):
        peer = lax.rem(w + s, W)
        return pltpu.make_async_remote_copy(
            src_ref=ctile,
            dst_ref=ctiles.at[w],
            send_sem=coef_send.at[s],
            recv_sem=coef_recv.at[W - s],
            device_id={"wall": peer},
            device_id_type=pl.DeviceIdType.MESH,
        )

    def coef_wait(s):
        pltpu.make_async_copy(ctile, ctiles.at[lax.rem(w + s, W)], coef_recv.at[s]).wait()

    slot = slots_s[lax.rem(step_s[0], slots_s.shape[0])]
    owner = lax.div(slot, stored)
    local = lax.rem(slot, stored)
    mine = owner == v
    before = owner < v
    shift = shift_s[0]

    def own_row(c, y):
        value = bs_v[0, c, y]
        for s in range(1, stored):
            value = jnp.where(local == s, bs_v[s, c, y], value)
        return value

    @pl.when(w < W - 1)
    def _():
        halo_up().start()

    @pl.when(w > 0)
    def _():
        halo_down().start()

    bs_in.wait()

    def each_row(k, body):
        for m in range(CHUNK_ROWS):
            for c in range(ncomp):
                body(c, k * CHUNK_ROWS + m)

    def shift_own(k, carry):
        def put(c, y):
            row = pltpu.roll(own_row(c, y).astype(jnp.float32), shift, 1)
            own_v[c, y] = row.astype(jnp.bfloat16)

        each_row(k, put)

        @pl.when(v == 0)
        def _():
            right_copy(k, own_v).start()

        @pl.when(v == V - 1)
        def _():
            left_copy(k, own_v).start()

        return carry

    lax.fori_loop(0, chunks, shift_own, 0)

    for s in range(1, W):
        coef_copy(s).start()

    q_in.wait()
    prev_in.wait()

    def prepare(n, c, y):
        mid = qpad[n, c, y + 1]
        above = qpad[n, c, y + 2]
        below = qpad[n, c, y]
        dx_v[n, c, y] = 0.5 * (pltpu.roll(mid, nx - 1, 0) - pltpu.roll(mid, 1, 0))
        dz_v[n, c, y] = 0.5 * (pltpu.roll(mid, nz - 1, 1) - pltpu.roll(mid, 1, 1))
        dy_v[n, c, y] = 0.5 * (above - below)
        loc[n, c, y] = (
            mid
            + (STEP_SIZE * OLD_WEIGHT) * prev_v[n, c, y].astype(jnp.float32)
            + VISCOUS_WEIGHT * (above - 2.0 * mid + below)
        )

    def prepare_chunk(p):
        def run(i, carry):
            for m in range(CHUNK_ROWS):
                prepare(lax.div(i, ncomp), lax.rem(i, ncomp), p * CHUNK_ROWS + m)
            return carry

        @pl.when((p == 0) & (w > 0))
        def _():
            halo_up().wait_recv()

        @pl.when((p == chunks - 1) & (w < W - 1))
        def _():
            halo_down().wait_recv()

        lax.fori_loop(0, fields, run, 0, unroll=PREP_UNROLL)

    fcar[...] = jnp.zeros_like(fcar)
    bcar[...] = jnp.zeros_like(bcar)

    def compute_chunk(k):
        for m in range(CHUNK_ROWS):
            y = k * CHUNK_ROWS + m
            base = []
            for c in range(ncomp):
                got = jnp.where(before, from_l[c, y], from_r[c, y])
                base.append(jnp.where(mine, own_v[c, y], got).astype(jnp.float32))
            d = 1.0 - gap_s[y]
            weight = tab_w[y]
            for n in range(nvec):
                for c in range(ncomp):
                    explicit = -(
                        base[0] * dx_v[n, c, y] + base[1] * dy_v[n, c, y] + base[2] * dz_v[n, c, y]
                    )
                    expl[n, c, y] = explicit.astype(jnp.bfloat16)
                    source = loc[n, c, y] + (STEP_SIZE * NEW_WEIGHT) * explicit
                    swept = source + d * fcar[n, c]
                    fcar[n, c] = swept
                    bcar[n, c] = bcar[n, c] + weight * swept
                    loc[n, c, y] = swept

    far = V - 1 - v

    def slot_step(t, carry):
        kl = t - HOP_LAG * v
        kr = t - HOP_LAG * far

        @pl.when((v > 0) & (kl >= 0) & (kl < chunks))
        def _():
            right_copy(kl, own_v).wait_recv()

            @pl.when(v < V - 1)
            def _():
                def put(c, y):
                    out_r[c, y] = jnp.where(mine, own_v[c, y], from_l[c, y])

                each_row(kl, put)
                right_copy(kl, out_r).start()

        @pl.when((v < V - 1) & (kr >= 0) & (kr < chunks))
        def _():
            left_copy(kr, own_v).wait_recv()

            @pl.when(v > 0)
            def _():
                def put(c, y):
                    out_l[c, y] = jnp.where(mine, own_v[c, y], from_r[c, y])

                each_row(kr, put)
                left_copy(kr, out_l).start()

        @pl.when(t < chunks)
        def _():
            prepare_chunk(jnp.where(t < 2, t + 1, jnp.where(t == 2, 0, t)))

        kc = jnp.minimum(kl, kr)

        @pl.when((kc >= 0) & (kc < chunks))
        def _():
            compute_chunk(kc)

        return carry

    lax.fori_loop(0, chunks + HOP_LAG * (V - 1), slot_step, 0)

    advec_out = pltpu.make_async_copy(expl, advec_hbm, out_sem.at[fields])
    advec_out.start()
    a_out = pltpu.make_async_copy(tabs.at[0], a_hbm, out_sem.at[fields + 3])
    a_out.start()
    c_out = pltpu.make_async_copy(tabs.at[1], c_hbm, out_sem.at[fields + 4])
    c_out.start()

    for s in range(1, W):
        coef_wait(s)

    def tail_response(m, total):
        j = W - 1 - m
        tile = ctiles[j]
        new = tile[2] + tile[1] * total * tile[0]
        return jnp.where(j > w, new, total)

    wide = nz // 128

    def widen(x):
        return jnp.concatenate([x] * wide, axis=-1)

    tail = widen(lax.fori_loop(0, W - 1, tail_response, jnp.zeros((nx, 128), jnp.float32)))
    gain = psi * tail

    for n in range(nvec):
        for c in range(ncomp):
            f = fcar[n, c]
            fsend[n, c] = f.astype(jnp.bfloat16)
            esend[n, c] = (bcar[n, c] + gain * f).astype(jnp.bfloat16)

    def carry_copy(s, src):
        return pltpu.make_async_remote_copy(
            src_ref=src,
            dst_ref=cin.at[w],
            send_sem=car_send.at[s],
            recv_sem=car_recv.at[W - s],
            device_id={"wall": lax.rem(w + s, W)},
            device_id_type=pl.DeviceIdType.MESH,
        )

    for s in range(1, W):

        @pl.when(w + s < W)
        def _():
            carry_copy(s, fsend).start()

        @pl.when(w + s >= W)
        def _():
            carry_copy(s, esend).start()

    def solve(i, carry):
        n = lax.div(i, ncomp)
        c = lax.rem(i, ncomp)
        later = jnp.zeros((nx, nz), jnp.float32)
        for y in range(rows - 1, -1, -1):
            later = tab_p[y] * loc[n, c, y] + tab_rho[y] * later
            loc[n, c, y] = later
        pltpu.make_async_copy(loc.at[n, c], part_hbm.at[n, c], out_sem.at[i]).start()
        return carry

    lax.fori_loop(0, fields, solve, 0)

    def forward_weight(m, prod):
        j = w - 1 - m
        tab_f[j] = prod
        return prod * widen(ctiles[j, 0])

    def backward_weight(m, prod):
        j = w + 1 + m
        tab_b[j] = prod
        return prod * widen(ctiles[j, 1])

    tab_f[...] = jnp.zeros_like(tab_f)
    tab_b[...] = jnp.zeros_like(tab_b)
    lax.fori_loop(0, w, forward_weight, one)
    lax.fori_loop(0, W - 1 - w, backward_weight, one)

    pairs = [(n, c) for n in range(nvec) for c in range(ncomp)]

    def gather(s, sums):
        j = lax.rem(w + s, W)
        pltpu.make_async_copy(fsend, cin.at[j], car_recv.at[s]).wait()
        wf, wb = tab_f[j], tab_b[j]
        new = []
        for (n, c), (f_in, b_in) in zip(pairs, sums):
            value = cin[j, n, c].astype(jnp.float32)
            new.append((f_in + wf * value, b_in + wb * value))
        return tuple(new)

    sums = tuple((one * 0.0, one * 0.0) for _ in pairs)
    sums = lax.fori_loop(1, W, gather, sums)
    for (n, c), (f_in, b_in) in zip(pairs, sums):
        edges[0, n, c] = f_in
        edges[1, n, c] = b_in + tail * (fcar[n, c] + phi * f_in)
    f_out = pltpu.make_async_copy(edges.at[0], f_hbm, out_sem.at[fields + 1])
    f_out.start()
    b_out = pltpu.make_async_copy(edges.at[1], b_hbm, out_sem.at[fields + 2])
    b_out.start()

    @pl.when(w < W - 1)
    def _():
        halo_up().wait_send()

    @pl.when(w > 0)
    def _():
        halo_down().wait_send()

    def drain(k, carry):
        @pl.when(v < V - 1)
        def _():
            right_copy(k, own_v).wait_send()

        @pl.when(v > 0)
        def _():
            left_copy(k, own_v).wait_send()

        return carry

    lax.fori_loop(0, chunks, drain, 0)
    for s in range(1, W):
        coef_copy(s).wait_send()
        carry_copy(s, fsend).wait_send()

    def drain_out(i, carry):
        n = lax.div(i, ncomp)
        c = lax.rem(i, ncomp)
        pltpu.make_async_copy(loc.at[n, c], part_hbm.at[n, c], out_sem.at[i]).wait()
        return carry

    lax.fori_loop(0, fields, drain_out, 0)
    advec_out.wait()
    f_out.wait()
    b_out.wait()
    a_out.wait()
    c_out.wait()


def combine(
    part, explicit, f_in, b_in, a_tab, c_tab, advanced, advection, x, e, f, b, a, c, in_sem, out_sem
):
    nvec, ncomp, rows = x.shape[:3]
    pairs = [(n, m) for n in range(nvec) for m in range(ncomp)]
    smalls = [
        pltpu.make_async_copy(src, dst, in_sem.at[k])
        for k, (src, dst) in enumerate(((f_in, f), (b_in, b), (a_tab, a), (c_tab, c)))
    ]
    loads = [
        pltpu.make_async_copy(part.at[n, m], x.at[n, m], in_sem.at[5 + k])
        for k, (n, m) in enumerate(pairs)
    ]
    stores = [
        pltpu.make_async_copy(x.at[n, m], advanced.at[n, m], out_sem.at[k])
        for k, (n, m) in enumerate(pairs)
    ]
    e_load = pltpu.make_async_copy(explicit, e, in_sem.at[4])
    e_store = pltpu.make_async_copy(e, advection, out_sem.at[len(pairs)])
    for copy in smalls + loads[:1] + [e_load] + loads[1:]:
        copy.start()
    for copy in smalls:
        copy.wait()
    for k, (n, m) in enumerate(pairs):
        loads[k].wait()
        for y in range(rows):
            x[n, m, y] = x[n, m, y] + a[y] * f[n, m] + c[y] * b[n, m]
        stores[k].start()
        if k == 1:
            e_load.wait()
            e_store.start()
    for copy in stores:
        copy.wait()
    e_store.wait()


def on_device(W, V, q, prev, bs, step, slots, shift, gap, piv, up):
    nvec, ncomp, rows, nx, nz = q.shape
    chunks = rows // CHUNK_ROWS
    field = (nvec, ncomp, rows, nx, nz)
    slab = (ncomp, rows, nx, nz)
    edge = (nvec, ncomp, nx, nz)
    hbm = pl.BlockSpec(memory_space=pltpu.HBM)
    f32, bf16 = jnp.float32, jnp.bfloat16
    dma = pltpu.SemaphoreType.DMA
    part, explicit, f_in, b_in, a_tab, c_tab = pl.pallas_call(
        functools.partial(kernel, W, V),
        out_shape=(
            jax.ShapeDtypeStruct(field, f32),
            jax.ShapeDtypeStruct(field, bf16),
            jax.ShapeDtypeStruct(edge, f32),
            jax.ShapeDtypeStruct(edge, f32),
            jax.ShapeDtypeStruct((rows, nx, nz), f32),
            jax.ShapeDtypeStruct((rows, nx, nz), f32),
        ),
        in_specs=[hbm] * 9,
        out_specs=(hbm,) * 6,
        scratch_shapes=[
            pltpu.SMEM(step.shape, step.dtype),
            pltpu.SMEM(slots.shape, slots.dtype),
            pltpu.SMEM(shift.shape, shift.dtype),
            pltpu.SMEM(gap.shape, gap.dtype),
            pltpu.SMEM(piv.shape, piv.dtype),
            pltpu.SMEM(up.shape, up.dtype),
            pltpu.VMEM(field, f32),
            pltpu.VMEM(field, f32),
            pltpu.VMEM(field, f32),
            pltpu.VMEM(slab, bf16),
            pltpu.VMEM((W, nx, nz), f32),
            pltpu.VMEM((W, nx, nz), f32),
            pltpu.VMEM((nvec, ncomp, rows + 2, nx, nz), f32),
            pltpu.VMEM(field, bf16),
            pltpu.VMEM(bs.shape, bf16),
            pltpu.VMEM(slab, bf16),
            pltpu.VMEM(slab, bf16),
            pltpu.VMEM(slab, bf16),
            pltpu.VMEM(slab, bf16),
            pltpu.VMEM(field, f32),
            pltpu.VMEM(field, bf16),
            pltpu.VMEM((2,) + edge, f32),
            pltpu.VMEM(edge, f32),
            pltpu.VMEM(edge, f32),
            pltpu.VMEM(edge, bf16),
            pltpu.VMEM(edge, bf16),
            pltpu.VMEM((W,) + edge, bf16),
            pltpu.VMEM((3, nx, 128), f32),
            pltpu.VMEM((W, 3, nx, 128), f32),
        ]
        + [pltpu.VMEM((rows, nx, nz), f32)] * 4
        + [
            pltpu.VMEM((2, rows, nx, nz), f32),
            dma((3,)),
            dma((6,)),
            dma((2,)),
            dma((2,)),
            dma((W,)),
            dma((W,)),
            dma((chunks,)),
            dma((chunks,)),
            dma((chunks,)),
            dma((chunks,)),
            dma((W,)),
            dma((W,)),
            dma((nvec * ncomp + 5,)),
        ],
        compiler_params=pltpu.CompilerParams(
            collective_id=0, has_side_effects=True, vmem_limit_bytes=63 * 1024 * 1024
        ),
    )(q, prev, bs, step, slots, shift, gap, piv, up)
    return pl.pallas_call(
        combine,
        out_shape=(jax.ShapeDtypeStruct(field, f32), jax.ShapeDtypeStruct(field, bf16)),
        in_specs=[hbm] * 6,
        out_specs=(hbm, hbm),
        scratch_shapes=[
            pltpu.VMEM(field, f32),
            pltpu.VMEM(field, bf16),
            pltpu.VMEM(edge, f32),
            pltpu.VMEM(edge, f32),
            pltpu.VMEM((rows, nx, nz), f32),
            pltpu.VMEM((rows, nx, nz), f32),
            dma((nvec * ncomp + 5,)),
            dma((nvec * ncomp + 1,)),
        ],
        compiler_params=pltpu.CompilerParams(vmem_limit_bytes=63 * 1024 * 1024),
    )(part, explicit, f_in, b_in, a_tab, c_tab)


def solution(mesh):
    W, V = mesh.shape["wall"], mesh.shape["vec"]
    field = P("vec", None, "wall", None, None)
    return jax.shard_map(
        functools.partial(on_device, W, V),
        mesh=mesh,
        in_specs=(field, field, field, P(), P(), P(), P("wall"), P("wall"), P("wall")),
        out_specs=(field, field),
        check_vma=False,
    )
```
